32 devices in a mesh: det: 8 (over y, x, core), row: 4 (over z).
Axes of the slice: x: 2, y: 2, z: 4, core: 2. Of those that a mesh axis runs over, the one named last changes fastest.
Arguments:
- coefficients: bfloat16 [8, 2048, 200], P('det', 'row'), may hold values from -1 to 1
- amplitudes: bfloat16 [8], P('det'), may hold values from -3 to 3
- plan: int32 [8, 2, 1], P('det'), may hold values 0 or 1
Outputs:
- density: float32 [2048, 2048], P('det', 'row')
The draws below stay inside these ranges and needn't reach their ends.
All inputs are finite; a program needn't handle non-finite values. No bound on the sum of `plan` on one device may be relied on, other than what follows from the above.
Results may differ from the reference program's by a relative error of at most 0.0024.
Values may be sent and summed in bfloat16 or wider, within the bound.
A program may use at most 64 MiB of HBM per device.

```python
import math
import jax
import jax.numpy as jnp
from jax import lax

NB = 2048
NOCC = 200
DET_DEV = 1
STEPS = 2
ORDER = 2
NDETS = 8
N_DET = 8


def draw_coefficients(key, part):
    shared = jax.random.normal(jax.random.fold_in(key, 11), (NB, NOCC), jnp.float32)
    basis, unused = jnp.linalg.qr(shared)
    spread = math.sqrt(0.3 / NB)
    weight_basis = math.sqrt(0.55)
    noise = jax.random.normal(jax.random.fold_in(key, 12), (NDETS, NB, NOCC), jnp.float32)
    values = weight_basis * basis[None, :, :] + spread * noise
    return jnp.clip(values, -1.0, 1.0).astype(jnp.bfloat16)


def touch_ends(array, key, least, top_value):
    spot = [jax.random.randint(jax.random.fold_in(key, axis), (), 0, length) for axis, length in enumerate(array.shape)]
    widest = array.shape.index(max(array.shape))
    next_to = spot[:widest] + [(spot[widest] + 1) % array.shape[widest]] + spot[widest + 1:]
    return array.at[tuple(spot)].set(least).at[tuple(next_to)].set(top_value)


def steps_of(key, dims, split, least, largest):
    factor_of = 1.0
    for dim, blocks in split:
        steps = jax.random.uniform(jax.random.fold_in(jax.random.fold_in(key, 6), dim), (blocks,), jnp.float32, least / len(split), largest / len(split))
        factor_of = factor_of * jnp.repeat(jnp.exp(steps), dims[dim] // blocks).reshape((-1,) + (1,) * (len(dims) - 1 - dim))
    return factor_of


def scatter_about(key, dims, width, limit, pieces=(), kind=jnp.bfloat16):
    result = width * jax.random.normal(key, dims, jnp.float32)
    if pieces:
        result = result * steps_of(key, dims, pieces, -0.22, 0.18)
    return jnp.clip(result, -limit, limit).astype(kind)


def setup_inputs(seed: int = 0) -> dict:
    arg_keys = jax.random.split(jax.random.key(seed), 4)
    return {
        "coefficients": draw_coefficients(jax.random.fold_in(arg_keys[3], 71), 0),
        "amplitudes": scatter_about(arg_keys[1], (NDETS,), 0.5, 3.0, ((0, 8),)),
        "plan": touch_ends((jax.random.randint(arg_keys[2], (NDETS, STEPS, DET_DEV), 0, 2) < 1).astype(jnp.int32), jax.random.fold_in(arg_keys[2], 1), 0, 1),
    }


def neumann(correlation):
    identity = jnp.eye(correlation.shape[-1], dtype=jnp.float32)
    remainder = identity - correlation
    inverse = identity + jnp.zeros_like(correlation)
    for level in range(ORDER):
        inverse = identity + jnp.einsum('...ab,...bc->...ac', remainder, inverse, precision=lax.Precision.HIGHEST)
    return inverse

def reference(coefficients, amplitudes, plan):
    blocks = coefficients.reshape(N_DET, DET_DEV, NB, NOCC)
    block_amps = amplitudes.astype(jnp.float32).reshape(N_DET, DET_DEV)
    masks = plan.astype(jnp.float32).reshape(N_DET, DET_DEV, STEPS, DET_DEV)

    def visit(total, block):
        ket = lax.dynamic_index_in_dim(blocks, block, 0, keepdims=False).astype(jnp.float32)
        ket_amps = lax.dynamic_index_in_dim(block_amps, block, 0, keepdims=False)
        ket_masks = lax.dynamic_index_in_dim(masks, block, 0, keepdims=False)
        accum = jnp.zeros((DET_DEV, NOCC, NB), jnp.float32)
        for step in range(STEPS):
            source = ((block - step) % N_DET).astype(jnp.int32)
            visitor = lax.dynamic_index_in_dim(blocks, source, 0, keepdims=False).astype(jnp.float32)
            visitor_amps = lax.dynamic_index_in_dim(block_amps, source, 0, keepdims=False)
            correlation = jnp.einsum('ina,jnb->ijab', visitor, ket, precision=lax.Precision.HIGHEST)
            weight = visitor_amps[:, None] * ket_amps[None, :] * ket_masks[:, step, :].T
            scaled = (weight[:, :, None, None] * neumann(correlation)).astype(jnp.bfloat16)
            accum = accum + jnp.einsum('ijba,ina->jbn', scaled.astype(jnp.float32), visitor, precision=lax.Precision.HIGHEST)
        folded = accum.astype(jnp.bfloat16).astype(jnp.float32)
        total = total + jnp.einsum('jmb,jbn->mn', ket, folded, precision=lax.Precision.HIGHEST)
        return (total, None)
    total, unused = lax.scan(visit, jnp.zeros((NB, NB), jnp.float32), jnp.arange(N_DET, dtype=jnp.int32))
    return total
```

```python
import functools

import jax
import jax.numpy as jnp
from jax import lax
from jax.experimental import pallas as pl
from jax.experimental.pallas import tpu as pltpu
from jax.sharding import PartitionSpec as P

ORDER = 2
F32 = jnp.float32
BF16 = jnp.bfloat16


def each(count, body):
    if count <= 8:
        for i in range(count):
            body(i)
    else:
        lax.fori_loop(0, count, lambda i, c: (body(i), c)[1], 0)


def inverse_of(correlation):
    size = correlation.shape[0]
    row = lax.broadcasted_iota(jnp.int32, (size, size), 0)
    col = lax.broadcasted_iota(jnp.int32, (size, size), 1)
    identity = jnp.where(row == col, 1.0, 0.0).astype(F32)
    remainder = identity - correlation
    inverse = identity + remainder
    for level in range(ORDER - 1):
        inverse = identity + jnp.dot(
            remainder, inverse, precision=lax.Precision.HIGHEST, preferred_element_type=F32
        )
    return inverse


def gram(a, b):
    return lax.dot_general(a, b, (((0,), (0,)), ((), ())), preferred_element_type=F32)


def against(a, b):
    return lax.dot_general(a, b, (((1,), (1,)), ((), ())), preferred_element_type=F32)


def kernel(
    n, ring, c_ref, amp_ref, mask_ref, out_ref,
    cw, vis, vamp, pw, s0, s1, pieces, folded,
    local_sem, cw_send, cw_recv, pw_send, pw_recv, vis_send, vis_recv,
    piece_send, piece_recv, chip_send, pair_send, folded_recv,
):
    det = lax.axis_index("det")
    row = lax.axis_index("row")
    rows = out_ref.shape[0]
    per_block = n // ring
    chips = n // 2
    chip, core = det // 2, lax.rem(det, 2)
    partner = chip * 2 + (1 - core)
    has_right, has_left = row < ring - 1, row > 0

    def remote(src, dst, send, recv, **where):
        return pltpu.make_async_remote_copy(
            src_ref=src, dst_ref=dst, send_sem=send, recv_sem=recv,
            device_id=where, device_id_type=pl.DeviceIdType.MESH,
        )

    keep = pltpu.make_async_copy(c_ref, cw.at[row], local_sem)
    keep.start()

    barrier = pltpu.get_barrier_semaphore()

    def greet(i):
        peer = lax.rem(det + 1 + i, n)
        pl.semaphore_signal(barrier, inc=1, device_id={"det": peer}, device_id_type=pl.DeviceIdType.MESH)

    each(n - 1, greet)

    @pl.when(has_right)
    def _():
        pl.semaphore_signal(barrier, inc=1, device_id={"row": row + 1}, device_id_type=pl.DeviceIdType.MESH)

    @pl.when(has_left)
    def _():
        pl.semaphore_signal(barrier, inc=1, device_id={"row": row - 1}, device_id_type=pl.DeviceIdType.MESH)

    pl.semaphore_wait(barrier, n - 1 + has_right.astype(jnp.int32) + has_left.astype(jnp.int32))

    def along(buf, sends, recvs, block, side):
        step = 1 if side == 0 else -1
        return remote(
            buf.at[block], buf.at[block], sends.at[block, side], recvs.at[block], row=row + step
        )

    def pass_on(buf, sends, recvs, block, side, wait=False):
        @pl.when(has_right if side == 0 else has_left)
        def _():
            copy = along(buf, sends, recvs, block, side)
            if wait:
                copy.wait_send()
            else:
                copy.start()

    def piece(block, k):
        target = block * per_block + k
        return target, remote(
            cw.at[block, pl.ds(k * rows, rows)], pieces.at[det],
            piece_send.at[block, k], piece_recv.at[det], det=target,
        )

    def hand_out(block, wait=False):
        def one(k):
            target, copy = piece(block, k)

            @pl.when(target != det)
            def _():
                if wait:
                    copy.wait_send()
                else:
                    copy.start()

        each(per_block, one)

    following = lax.rem(det + 1, n)
    visit = remote(c_ref, vis, vis_send.at[0], vis_recv.at[0], det=following)
    visit_amp = remote(amp_ref, vamp, vis_send.at[1], vis_recv.at[1], det=following)
    keep.wait()
    for side in (0, 1):
        pass_on(cw, cw_send, cw_recv, row, side)
    visit.start()
    visit_amp.start()
    s0[...] = gram(c_ref[...], c_ref[...])
    visit.wait_recv()
    hand_out(row)
    s1[...] = gram(vis[...], c_ref[...])
    pw[row] = s1[...]
    for side in (0, 1):
        pass_on(pw, pw_send, pw_recv, row, side)

    for distance in range(1, ring):
        for side in (0, 1):
            block = row - distance if side == 0 else row + distance

            @pl.when((block >= 0) & (block < ring))
            def _():
                along(cw, cw_send, cw_recv, block, side).wait_recv()
                pass_on(cw, cw_send, cw_recv, block, side)
                hand_out(block)
                s0[...] += gram(cw[block], cw[block])

        for side in (0, 1):
            block = row - distance if side == 0 else row + distance

            @pl.when((block >= 0) & (block < ring))
            def _():
                along(pw, pw_send, pw_recv, block, side).wait_recv()
                pass_on(pw, pw_send, pw_recv, block, side)
                s1[...] += pw[block]

    visit_amp.wait_recv()
    amp = amp_ref[0:1, 0:1]
    weight = amp * amp * mask_ref[0, 0:1, 0:1]
    scaled = (weight * inverse_of(s0[...])).astype(BF16)
    total = against(scaled, c_ref[...])
    weight = vamp[0:1, 0:1] * amp * mask_ref[1, 0:1, 0:1]
    scaled = (weight * inverse_of(s1[...])).astype(BF16)
    folded[det] = (total + against(scaled, vis[...])).astype(BF16)

    def to_chip(i):
        target = lax.rem(chip + 1 + i, chips) * 2 + core
        return remote(folded.at[det], folded.at[det], chip_send.at[i], folded_recv.at[det], det=target)

    def to_pair(source):
        return remote(
            folded.at[source], folded.at[source], pair_send.at[source], folded_recv.at[source], det=partner
        )

    each(chips - 1, lambda i: to_chip(i).start())
    to_pair(det).start()

    def landed(source):
        to_pair(source).wait_recv()

    def add(source):
        remote(
            cw.at[0, pl.ds(0, rows)], pieces.at[source], piece_send.at[0, 0], piece_recv.at[source], det=partner
        ).wait_recv()
        out_ref[...] += jnp.dot(pieces[source], folded[source], preferred_element_type=F32)

    own_block, own_part = det // per_block, lax.rem(det, per_block)
    mine = cw[own_block, pl.ds(pl.multiple_of(own_part * rows, rows), rows)]
    out_ref[...] = jnp.dot(mine, folded[det], preferred_element_type=F32)
    landed(partner)
    add(partner)

    def relay(i):
        other = lax.rem(chip + chips - 1 - i, chips) * 2
        landed(other + core)
        to_pair(other + core).start()
        add(other + core)

    def relayed(i):
        other = lax.rem(chip + chips - 1 - i, chips) * 2
        landed(other + 1 - core)
        add(other + 1 - core)

    each(chips - 1, relay)
    each(chips - 1, relayed)

    visit.wait_send()
    visit_amp.wait_send()
    for side in (0, 1):
        pass_on(cw, cw_send, cw_recv, row, side, wait=True)
        pass_on(pw, pw_send, pw_recv, row, side, wait=True)
    hand_out(row, wait=True)
    for distance in range(1, ring):
        for side in (0, 1):
            block = row - distance if side == 0 else row + distance

            @pl.when((block >= 0) & (block < ring))
            def _():
                pass_on(cw, cw_send, cw_recv, block, side, wait=True)
                pass_on(pw, pw_send, pw_recv, block, side, wait=True)
                hand_out(block, wait=True)

    each(chips - 1, lambda i: to_chip(i).wait_send())
    to_pair(det).wait_send()
    each(chips - 1, lambda i: to_pair(lax.rem(chip + chips - 1 - i, chips) * 2 + core).wait_send())


def on_device(coefficients, amplitudes, plan):
    n, ring = lax.axis_size("det"), lax.axis_size("row")
    block = coefficients[0]
    size, orbitals = block.shape
    steps = plan.shape[1]
    if coefficients.shape[0] != 1 or steps != 2:
        raise ValueError("unsupported sizes")
    rows = size * ring // n
    amp = jnp.broadcast_to(amplitudes.astype(F32)[:, None], (8, 128))
    masks = jnp.broadcast_to(plan.astype(F32).reshape(steps, 1, 1), (steps, 8, 128))
    dma = pltpu.SemaphoreType.DMA
    return pl.pallas_call(
        functools.partial(kernel, n, ring),
        out_shape=jax.ShapeDtypeStruct((rows, size), F32),
        in_specs=[pl.BlockSpec(memory_space=pltpu.VMEM)] * 3,
        out_specs=pl.BlockSpec(memory_space=pltpu.VMEM),
        scratch_shapes=[
            pltpu.VMEM((ring, size, orbitals), BF16),
            pltpu.VMEM((size, orbitals), BF16),
            pltpu.VMEM((8, 128), F32),
            pltpu.VMEM((ring, orbitals, orbitals), F32),
            pltpu.VMEM((orbitals, orbitals), F32),
            pltpu.VMEM((orbitals, orbitals), F32),
            pltpu.VMEM((n, rows, orbitals), BF16),
            pltpu.VMEM((n, orbitals, size), BF16),
            dma, dma((ring, 2)), dma((ring,)), dma((ring, 2)), dma((ring,)), dma((2,)), dma((2,)),
            dma((ring, n // ring)), dma((n,)), dma((n // 2,)), dma((n,)), dma((n,)),
        ],
        compiler_params=pltpu.CompilerParams(
            collective_id=0, has_side_effects=True, vmem_limit_bytes=60 * 1024 * 1024
        ),
    )(block, amp, masks)


def solution(mesh):
    placed = (P("det", "row", None), P("det"), P("det", None, None))
    return jax.shard_map(
        on_device, mesh=mesh, in_specs=placed, out_specs=P("det", "row"), check_vma=False
    )
```

```python
import functools

import jax
import jax.numpy as jnp
from jax import lax
from jax.experimental import pallas as pl
from jax.experimental.pallas import tpu as pltpu
from jax.sharding import PartitionSpec as P

ORDER = 2
F32 = jnp.float32
BF16 = jnp.bfloat16


def each(count, body):
    if count <= 8:
        for i in range(count):
            body(i)
    else:
        lax.fori_loop(0, count, lambda i, c: (body(i), c)[1], 0)


def inverse_of(correlation):
    size = correlation.shape[0]
    row = lax.broadcasted_iota(jnp.int32, (size, size), 0)
    col = lax.broadcasted_iota(jnp.int32, (size, size), 1)
    identity = jnp.where(row == col, 1.0, 0.0).astype(F32)
    remainder = identity - correlation
    inverse = identity + remainder
    for level in range(ORDER - 1):
        inverse = identity + jnp.dot(
            remainder, inverse, precision=lax.Precision.HIGHEST, preferred_element_type=F32
        )
    return inverse


def gram(a, b):
    return lax.dot_general(a, b, (((0,), (0,)), ((), ())), preferred_element_type=F32)


def against(a, b):
    return lax.dot_general(a, b, (((1,), (1,)), ((), ())), preferred_element_type=F32)


def parts_of(size, count):
    step = -(-size // (8 * count)) * 8
    return [(start, min(step, size - start)) for start in range(0, size, step)]


def kernel(
    n, ring, c_ref, amp_ref, plan_ref, out_ref,
    cw, vis, amps, own, sum_in, sum_out, s0, pieces, folded, wide,
    local_sem, cw_send, cw_recv, sum_send, sum_recv, vis_send, vis_recv,
    piece_send, piece_recv, chip_send, pair_send, folded_recv,
):
    det = lax.axis_index("det")
    row = lax.axis_index("row")
    rows = out_ref.shape[0]
    width = pieces.shape[2]
    per_block = n // ring
    chips = n // 2
    chip, core = det // 2, lax.rem(det, 2)
    partner = chip * 2 + (1 - core)
    has_right, has_left = row < ring - 1, row > 0
    toward = (has_right, has_left)
    chunks = parts_of(own.shape[0], 4)

    def remote(src, dst, send, recv, **where):
        return pltpu.make_async_remote_copy(
            src_ref=src, dst_ref=dst, send_sem=send, recv_sem=recv,
            device_id=where, device_id_type=pl.DeviceIdType.MESH,
        )

    keep = pltpu.make_async_copy(c_ref, cw.at[row], local_sem)
    keep.start()

    barrier = pltpu.get_barrier_semaphore()

    def greet(i):
        peer = lax.rem(det + 1 + i, n)
        pl.semaphore_signal(barrier, inc=1, device_id={"det": peer}, device_id_type=pl.DeviceIdType.MESH)

    each(n - 1, greet)

    for side in (0, 1):

        @pl.when(toward[side])
        def _():
            peer = row + 1 - 2 * side
            pl.semaphore_signal(barrier, inc=1, device_id={"row": peer}, device_id_type=pl.DeviceIdType.MESH)

    amps[0] = jnp.broadcast_to(amp_ref[...].astype(F32), amps.shape[1:])
    pl.semaphore_wait(barrier, n - 1 + has_right.astype(jnp.int32) + has_left.astype(jnp.int32))

    def along(block, side):
        return remote(
            cw.at[block], cw.at[block], cw_send.at[block, side], cw_recv.at[block], row=row + 1 - 2 * side
        )

    def pass_on(block, side, wait=False):
        @pl.when(toward[side])
        def _():
            copy = along(block, side)
            if wait:
                copy.wait_send()
            else:
                copy.start()

    def chunk_copy(k, side):
        span = pl.ds(*chunks[k])
        return remote(
            sum_out.at[side, span], sum_in.at[side, span], sum_send.at[side, k], sum_recv.at[side, k],
            row=row + 1 - 2 * side,
        )

    def sums(side, first):
        for k, (start, length) in enumerate(chunks):
            span = pl.ds(start, length)
            if first:
                sum_in[side, span] = jnp.zeros((length, own.shape[1]), F32)
                sum_out[side, span] = own[span]
            else:
                chunk_copy(k, side).wait_recv()
                sum_out[side, span] = own[span] + sum_in[side, span]

            @pl.when(toward[side])
            def _():
                chunk_copy(k, side).start()

    def piece(block, k):
        target = block * per_block + k
        start = pl.multiple_of(k * rows // width * width, width)
        return target, remote(
            cw.at[block, :, pl.ds(start, width)], pieces.at[det],
            piece_send.at[block, k], piece_recv.at[det], det=target,
        )

    def hand_out(block, wait=False):
        def one(k):
            target, copy = piece(block, k)

            @pl.when(target != det)
            def _():
                if wait:
                    copy.wait_send()
                else:
                    copy.start()

        each(per_block, one)

    following = lax.rem(det + 1, n)
    visit = remote(c_ref, vis, vis_send.at[0], vis_recv.at[0], det=following)
    visit_amp = remote(amps.at[0], amps.at[1], vis_send.at[1], vis_recv.at[1], det=following)
    visit.start()
    visit_amp.start()
    keep.wait()
    for side in (0, 1):
        pass_on(row, side)
    s0[...] = against(c_ref[...], c_ref[...])
    visit.wait_recv()
    own[...] = against(vis[...], c_ref[...])

    @pl.when(row == 0)
    def _():
        sums(0, True)

    @pl.when(row == ring - 1)
    def _():
        sums(1, True)

    hand_out(row)

    def arrive(distance):
        for side in (0, 1):
            block = row - distance if side == 0 else row + distance

            @pl.when((block >= 0) & (block < ring))
            def _():
                along(block, side).wait_recv()
                pass_on(block, side)
                hand_out(block)
                s0[...] += against(cw[block], cw[block])

    def gather_sums(distance):
        @pl.when(row == distance)
        def _():
            sums(0, False)

        @pl.when(row == ring - 1 - distance)
        def _():
            sums(1, False)

    for distance in range(1, ring - 1):
        arrive(distance)
        gather_sums(distance)
    arrive(ring - 1)
    visit_amp.wait_recv()
    amp = amps[0, 0:1, 0:1]
    masks = plan_ref[...].astype(F32)
    weight = amp * amp * masks[0:1, 0:1]
    scaled = (weight * inverse_of(s0[...])).astype(BF16)
    total = jnp.dot(scaled, c_ref[...], preferred_element_type=F32)
    gather_sums(ring - 1)
    weight = amps[1, 0:1, 0:1] * amp * masks[1:2, 0:1]
    correlation = own[...] + sum_in[0] + sum_in[1]
    scaled = (weight * inverse_of(correlation)).astype(BF16)
    total = total + jnp.dot(scaled, vis[...], preferred_element_type=F32)
    folded[det] = total.astype(BF16)

    def to_chip(i):
        target = lax.rem(chip + 1 + i, chips) * 2 + core
        return remote(folded.at[det], folded.at[det], chip_send.at[i], folded_recv.at[det], det=target)

    def to_pair(source):
        return remote(
            folded.at[source], folded.at[source], pair_send.at[source], folded_recv.at[source], det=partner
        )

    each(chips - 1, lambda i: to_chip(i).start())
    to_pair(det).start()

    def landed(source):
        to_pair(source).wait_recv()

    sink = out_ref if width == rows else wide

    def add(source):
        remote(
            cw.at[0, :, pl.ds(0, width)], pieces.at[source], piece_send.at[0, 0], piece_recv.at[source],
            det=partner,
        ).wait_recv()
        sink[...] += gram(pieces[source], folded[source])

    own_start = lax.rem(det, per_block) * rows // width * width
    mine = cw[det // per_block, :, pl.ds(pl.multiple_of(own_start, width), width)]
    sink[...] = gram(mine, folded[det])
    landed(partner)
    add(partner)

    def relay(i):
        other = lax.rem(chip + chips - 1 - i, chips) * 2
        landed(other + core)
        to_pair(other + core).start()
        add(other + core)

    def relayed(i):
        other = lax.rem(chip + chips - 1 - i, chips) * 2
        landed(other + 1 - core)
        add(other + 1 - core)

    each(chips - 1, relay)
    each(chips - 1, relayed)
    if width != rows:
        out_ref[...] = wide[pl.ds(pl.multiple_of(lax.rem(det * rows, width), rows), rows)]

    visit.wait_send()
    visit_amp.wait_send()
    for side in (0, 1):
        pass_on(row, side, wait=True)

        @pl.when(toward[side])
        def _():
            for k in range(len(chunks)):
                chunk_copy(k, side).wait_send()

    hand_out(row, wait=True)
    for distance in range(1, ring):
        for side in (0, 1):
            block = row - distance if side == 0 else row + distance

            @pl.when((block >= 0) & (block < ring))
            def _():
                pass_on(block, side, wait=True)
                hand_out(block, wait=True)

    each(chips - 1, lambda i: to_chip(i).wait_send())
    to_pair(det).wait_send()
    each(chips - 1, lambda i: to_pair(lax.rem(chip + chips - 1 - i, chips) * 2 + core).wait_send())


def on_device(coefficients, amplitudes, plan):
    n, ring = lax.axis_size("det"), lax.axis_size("row")
    if coefficients.shape[0] != 1 or plan.shape[1] != 2:
        raise ValueError("unsupported sizes")
    block = jnp.swapaxes(coefficients, 1, 2)[0]
    orbitals, size = block.shape
    rows = size * ring // n
    width = max(rows, 128)
    dma = pltpu.SemaphoreType.DMA
    return pl.pallas_call(
        functools.partial(kernel, n, ring),
        out_shape=jax.ShapeDtypeStruct((rows, size), F32),
        in_specs=[pl.BlockSpec(memory_space=pltpu.VMEM)] * 3,
        out_specs=pl.BlockSpec(memory_space=pltpu.VMEM),
        scratch_shapes=[
            pltpu.VMEM((ring, orbitals, size), BF16),
            pltpu.VMEM((orbitals, size), BF16),
            pltpu.VMEM((2, 8, 128), F32),
            pltpu.VMEM((orbitals, orbitals), F32),
            pltpu.VMEM((2, orbitals, orbitals), F32),
            pltpu.VMEM((2, orbitals, orbitals), F32),
            pltpu.VMEM((orbitals, orbitals), F32),
            pltpu.VMEM((n, orbitals, width), BF16),
            pltpu.VMEM((n, orbitals, size), BF16),
            pltpu.VMEM((width, size) if width != rows else (8, 128), F32),
            dma, dma((ring, 2)), dma((ring,)), dma((2, 4)), dma((2, 4)), dma((2,)), dma((2,)),
            dma((ring, n // ring)), dma((n,)), dma((n // 2,)), dma((n,)), dma((n,)),
        ],
        compiler_params=pltpu.CompilerParams(
            collective_id=0, has_side_effects=True, vmem_limit_bytes=60 * 1024 * 1024
        ),
    )(block, amplitudes.reshape(1, 1), plan.reshape(2, 1))


def solution(mesh):
    placed = (P("det", "row", None), P("det"), P("det", None, None))
    return jax.shard_map(
        on_device, mesh=mesh, in_specs=placed, out_specs=P("det", "row"), check_vma=False
    )
```

```python
import functools

import jax
import jax.numpy as jnp
from jax import lax
from jax.experimental import pallas as pl
from jax.experimental.pallas import tpu as pltpu
from jax.sharding import PartitionSpec as P

ORDER = 2
F32 = jnp.float32
BF16 = jnp.bfloat16


def each(count, body):
    if count <= 8:
        for i in range(count):
            body(i)
    else:
        lax.fori_loop(0, count, lambda i, c: (body(i), c)[1], 0)


def inverse_of(correlation):
    size = correlation.shape[0]
    row = lax.broadcasted_iota(jnp.int32, (size, size), 0)
    col = lax.broadcasted_iota(jnp.int32, (size, size), 1)
    identity = jnp.where(row == col, 1.0, 0.0).astype(F32)
    remainder = identity - correlation
    inverse = identity + remainder
    for level in range(ORDER - 1):
        inverse = identity + jnp.dot(
            remainder, inverse, precision=lax.Precision.HIGHEST, preferred_element_type=F32
        )
    return inverse


def gram(a, b):
    return lax.dot_general(a, b, (((0,), (0,)), ((), ())), preferred_element_type=F32)


def against(a, b):
    return lax.dot_general(a, b, (((1,), (1,)), ((), ())), preferred_element_type=F32)


def parts_of(size, count):
    step = -(-size // (8 * count)) * 8
    return [(start, min(step, size - start)) for start in range(0, size, step)]


def kernel(
    n, ring, c_ref, amp_ref, plan_ref, out_ref,
    cw, vis, amps, own, sum_in, sum_out, pieces, folded, wide,
    local_sem, cw_send, cw_recv, sum_send, sum_recv, vis_send, vis_recv,
    piece_send, piece_recv, chip_send, pair_send, folded_recv,
):
    det = lax.axis_index("det")
    row = lax.axis_index("row")
    rows = out_ref.shape[0]
    width = pieces.shape[2]
    per_block = n // ring
    chips = n // 2
    chip, core = det // 2, lax.rem(det, 2)
    partner = chip * 2 + (1 - core)
    has_right, has_left = row < ring - 1, row > 0
    toward = (has_right, has_left)
    chunks = parts_of(own.shape[1], 4)

    def remote(src, dst, send, recv, **where):
        return pltpu.make_async_remote_copy(
            src_ref=src, dst_ref=dst, send_sem=send, recv_sem=recv,
            device_id=where, device_id_type=pl.DeviceIdType.MESH,
        )

    keep = pltpu.make_async_copy(c_ref, cw.at[row], local_sem)
    keep.start()

    barrier = pltpu.get_barrier_semaphore()

    def greet(i):
        peer = lax.rem(det + 1 + i, n)
        pl.semaphore_signal(barrier, inc=1, device_id={"det": peer}, device_id_type=pl.DeviceIdType.MESH)

    each(n - 1, greet)

    for side in (0, 1):

        @pl.when(toward[side])
        def _():
            peer = row + 1 - 2 * side
            pl.semaphore_signal(barrier, inc=1, device_id={"row": peer}, device_id_type=pl.DeviceIdType.MESH)

    amps[0] = jnp.broadcast_to(amp_ref[...].astype(F32), amps.shape[1:])
    pl.semaphore_wait(barrier, n - 1 + has_right.astype(jnp.int32) + has_left.astype(jnp.int32))

    def along(block, side, half):
        span = cw.at[block, :, pl.ds(half * (cw.shape[2] // 2), cw.shape[2] // 2)]
        return remote(
            span, span, cw_send.at[block, side, half], cw_recv.at[block, half], row=row + 1 - 2 * side
        )

    def pass_on(block, side, half, wait=False):
        @pl.when(toward[side])
        def _():
            copy = along(block, side, half)
            if wait:
                copy.wait_send()
            else:
                copy.start()

    def chunk_copy(which, k, side):
        span = pl.ds(*chunks[k])
        return remote(
            sum_out.at[which, side, span], sum_in.at[which, side, span],
            sum_send.at[which, side, k], sum_recv.at[which, side, k], row=row + 1 - 2 * side,
        )

    def sums(which, side, first):
        for k, (start, length) in enumerate(chunks):
            span = pl.ds(start, length)
            if first:
                sum_in[which, side, span] = jnp.zeros((length, own.shape[2]), F32)
                sum_out[which, side, span] = own[which, span]
            else:
                chunk_copy(which, k, side).wait_recv()
                sum_out[which, side, span] = own[which, span] + sum_in[which, side, span]

            @pl.when(toward[side])
            def _():
                chunk_copy(which, k, side).start()

    def open_sums(which):
        @pl.when(row == 0)
        def _():
            sums(which, 0, True)

        @pl.when(row == ring - 1)
        def _():
            sums(which, 1, True)

    def piece(block, k):
        target = block * per_block + k
        start = pl.multiple_of(k * rows // width * width, width)
        return target, remote(
            cw.at[block, :, pl.ds(start, width)], pieces.at[det],
            piece_send.at[block, k], piece_recv.at[det], det=target,
        )

    def hand_out(block, half, wait=False):
        def one(part):
            target, copy = piece(block, half * (per_block // 2) + part)

            @pl.when(target != det)
            def _():
                if wait:
                    copy.wait_send()
                else:
                    copy.start()

        each(per_block // 2, one)

    following = lax.rem(det + 1, n)
    visit = remote(c_ref, vis, vis_send.at[0], vis_recv.at[0], det=following)
    visit_amp = remote(amps.at[0], amps.at[1], vis_send.at[1], vis_recv.at[1], det=following)
    visit.start()
    visit_amp.start()
    keep.wait()
    for half in (0, 1):
        for side in (0, 1):
            pass_on(row, side, half)
    own[0] = against(c_ref[...], c_ref[...])
    open_sums(0)
    visit.wait_recv()
    own[1] = against(vis[...], c_ref[...])
    open_sums(1)
    for half in (0, 1):
        hand_out(row, half)

    def arrive(distance):
        for half in (0, 1):
            for side in (0, 1):
                block = row - distance if side == 0 else row + distance

                @pl.when((block >= 0) & (block < ring))
                def _():
                    along(block, side, half).wait_recv()
                    pass_on(block, side, half)
                    hand_out(block, half)

    def gather_sums(distance):
        for which in (0, 1):

            @pl.when(row == distance)
            def _():
                sums(which, 0, False)

            @pl.when(row == ring - 1 - distance)
            def _():
                sums(which, 1, False)

    arrive(1)
    gather_sums(1)
    for distance in range(2, ring - 1):
        gather_sums(distance)
        arrive(distance)
    gather_sums(ring - 1)
    visit_amp.wait_recv()
    amp = amps[0, 0:1, 0:1]
    masks = plan_ref[...].astype(F32)

    def scaled(which):
        weight = amps[which, 0:1, 0:1] * amp * masks[which:which + 1, 0:1]
        correlation = own[which] + sum_in[which, 0] + sum_in[which, 1]
        return (weight * inverse_of(correlation)).astype(BF16)

    total = jnp.dot(scaled(0), c_ref[...], preferred_element_type=F32)
    total = total + jnp.dot(scaled(1), vis[...], preferred_element_type=F32)
    folded[det] = total.astype(BF16)

    def to_chip(i):
        target = lax.rem(chip + 1 + i, chips) * 2 + core
        return remote(folded.at[det], folded.at[det], chip_send.at[i], folded_recv.at[det], det=target)

    def to_pair(source):
        return remote(
            folded.at[source], folded.at[source], pair_send.at[source], folded_recv.at[source], det=partner
        )

    each(chips - 1, lambda i: to_chip(i).start())
    to_pair(det).start()
    arrive(ring - 1)

    def landed(source):
        to_pair(source).wait_recv()

    sink = out_ref if width == rows else wide

    def add(source):
        remote(
            cw.at[0, :, pl.ds(0, width)], pieces.at[source], piece_send.at[0, 0], piece_recv.at[source],
            det=partner,
        ).wait_recv()
        sink[...] += gram(pieces[source], folded[source])

    own_start = lax.rem(det, per_block) * rows // width * width
    mine = cw[det // per_block, :, pl.ds(pl.multiple_of(own_start, width), width)]
    sink[...] = gram(mine, folded[det])
    landed(partner)
    add(partner)

    def relay(i):
        other = lax.rem(chip + chips - 1 - i, chips) * 2
        landed(other + core)
        to_pair(other + core).start()
        add(other + core)

    def relayed(i):
        other = lax.rem(chip + chips - 1 - i, chips) * 2
        landed(other + 1 - core)
        add(other + 1 - core)

    each(chips - 1, relay)
    each(chips - 1, relayed)
    if width != rows:
        out_ref[...] = wide[pl.ds(pl.multiple_of(lax.rem(det * rows, width), rows), rows)]

    visit.wait_send()
    visit_amp.wait_send()
    for side in (0, 1):

        @pl.when(toward[side])
        def _():
            for which in (0, 1):
                for k in range(len(chunks)):
                    chunk_copy(which, k, side).wait_send()

    for half in (0, 1):
        for side in (0, 1):
            pass_on(row, side, half, wait=True)
        hand_out(row, half, wait=True)
        for distance in range(1, ring):
            for side in (0, 1):
                block = row - distance if side == 0 else row + distance

                @pl.when((block >= 0) & (block < ring))
                def _():
                    pass_on(block, side, half, wait=True)
                    hand_out(block, half, wait=True)

    each(chips - 1, lambda i: to_chip(i).wait_send())
    to_pair(det).wait_send()
    each(chips - 1, lambda i: to_pair(lax.rem(chip + chips - 1 - i, chips) * 2 + core).wait_send())


def on_device(coefficients, amplitudes, plan):
    n, ring = lax.axis_size("det"), lax.axis_size("row")
    if coefficients.shape[0] != 1 or plan.shape[1] != 2:
        raise ValueError("unsupported sizes")
    block = jnp.swapaxes(coefficients, 1, 2)[0]
    orbitals, size = block.shape
    rows = size * ring // n
    width = max(rows, 128)
    dma = pltpu.SemaphoreType.DMA
    return pl.pallas_call(
        functools.partial(kernel, n, ring),
        out_shape=jax.ShapeDtypeStruct((rows, size), F32),
        in_specs=[pl.BlockSpec(memory_space=pltpu.VMEM)] * 3,
        out_specs=pl.BlockSpec(memory_space=pltpu.VMEM),
        scratch_shapes=[
            pltpu.VMEM((ring, orbitals, size), BF16),
            pltpu.VMEM((orbitals, size), BF16),
            pltpu.VMEM((2, 8, 128), F32),
            pltpu.VMEM((2, orbitals, orbitals), F32),
            pltpu.VMEM((2, 2, orbitals, orbitals), F32),
            pltpu.VMEM((2, 2, orbitals, orbitals), F32),
            pltpu.VMEM((n, orbitals, width), BF16),
            pltpu.VMEM((n, orbitals, size), BF16),
            pltpu.VMEM((width, size) if width != rows else (8, 128), F32),
            dma, dma((ring, 2, 2)), dma((ring, 2)), dma((2, 2, 4)), dma((2, 2, 4)), dma((2,)), dma((2,)),
            dma((ring, n // ring)), dma((n,)), dma((n // 2,)), dma((n,)), dma((n,)),
        ],
        compiler_params=pltpu.CompilerParams(
            collective_id=0, has_side_effects=True, vmem_limit_bytes=60 * 1024 * 1024
        ),
    )(block, amplitudes.reshape(1, 1), plan.reshape(2, 1))


def solution(mesh):
    placed = (P("det", "row", None), P("det"), P("det", None, None))
    return jax.shard_map(
        on_device, mesh=mesh, in_specs=placed, out_specs=P("det", "row"), check_vma=False
    )
```

```python
import functools

import jax
import jax.numpy as jnp
from jax import lax
from jax.experimental import pallas as pl
from jax.experimental.pallas import tpu as pltpu
from jax.sharding import PartitionSpec as P

ORDER = 2
F32 = jnp.float32
BF16 = jnp.bfloat16


def each(count, body):
    if count <= 8:
        for i in range(count):
            body(i)
    else:
        lax.fori_loop(0, count, lambda i, c: (body(i), c)[1], 0)


def inverse_of(correlation):
    size = correlation.shape[0]
    row = lax.broadcasted_iota(jnp.int32, (size, size), 0)
    col = lax.broadcasted_iota(jnp.int32, (size, size), 1)
    identity = jnp.where(row == col, 1.0, 0.0).astype(F32)
    remainder = identity - correlation
    inverse = identity + remainder
    for level in range(ORDER - 1):
        inverse = identity + jnp.dot(
            remainder, inverse, precision=lax.Precision.HIGHEST, preferred_element_type=F32
        )
    return inverse


def gram(a, b):
    return lax.dot_general(a, b, (((0,), (0,)), ((), ())), preferred_element_type=F32)


def against(a, b):
    return lax.dot_general(a, b, (((1,), (1,)), ((), ())), preferred_element_type=F32)


def parts_of(size, count):
    step = -(-size // (8 * count)) * 8
    return [(start, min(step, size - start)) for start in range(0, size, step)]


def kernel(
    n, ring, c_ref, amp_ref, plan_ref, out_ref,
    cw, vis, amps, own, sum_in, sum_out, s0, pieces, folded, wide,
    local_sem, cw_send, cw_recv, sum_send, sum_recv, vis_send, vis_recv,
    piece_send, piece_recv, chip_send, pair_send, folded_recv,
):
    det = lax.axis_index("det")
    row = lax.axis_index("row")
    rows = out_ref.shape[0]
    width = pieces.shape[2]
    per_block = n // ring
    chips = n // 2
    chip, core = det // 2, lax.rem(det, 2)
    partner = chip * 2 + (1 - core)
    has_right, has_left = row < ring - 1, row > 0
    toward = (has_right, has_left)
    chunks = parts_of(own.shape[0], 4)

    def remote(src, dst, send, recv, **where):
        return pltpu.make_async_remote_copy(
            src_ref=src, dst_ref=dst, send_sem=send, recv_sem=recv,
            device_id=where, device_id_type=pl.DeviceIdType.MESH,
        )

    keep = pltpu.make_async_copy(c_ref, cw.at[row], local_sem)
    keep.start()

    barrier = pltpu.get_barrier_semaphore()

    def greet(i):
        peer = lax.rem(det + 1 + i, n)
        pl.semaphore_signal(barrier, inc=1, device_id={"det": peer}, device_id_type=pl.DeviceIdType.MESH)

    each(n - 1, greet)

    for side in (0, 1):

        @pl.when(toward[side])
        def _():
            peer = row + 1 - 2 * side
            pl.semaphore_signal(barrier, inc=1, device_id={"row": peer}, device_id_type=pl.DeviceIdType.MESH)

    amps[0] = jnp.broadcast_to(amp_ref[...].astype(F32), amps.shape[1:])
    pl.semaphore_wait(barrier, n - 1 + has_right.astype(jnp.int32) + has_left.astype(jnp.int32))

    halves = parts_of(own.shape[0], 2)

    def along(block, side, half):
        span = cw.at[block, pl.ds(*halves[half])]
        return remote(
            span, span, cw_send.at[block, side, half], cw_recv.at[block, half], row=row + 1 - 2 * side
        )

    def pass_on(block, side, half, wait=False):
        @pl.when(toward[side])
        def _():
            copy = along(block, side, half)
            if wait:
                copy.wait_send()
            else:
                copy.start()

    def chunk_copy(k, side):
        span = pl.ds(*chunks[k])
        return remote(
            sum_out.at[side, span], sum_in.at[side, span], sum_send.at[side, k], sum_recv.at[side, k],
            row=row + 1 - 2 * side,
        )

    def sums(side, first):
        for k, (start, length) in enumerate(chunks):
            span = pl.ds(start, length)
            if first:
                sum_in[side, span] = jnp.zeros((length, own.shape[1]), F32)
                sum_out[side, span] = own[span]
            else:
                chunk_copy(k, side).wait_recv()
                sum_out[side, span] = own[span] + sum_in[side, span]

            @pl.when(toward[side])
            def _():
                chunk_copy(k, side).start()

    def piece(block, k):
        target = block * per_block + k
        start = pl.multiple_of(k * rows // width * width, width)
        return target, remote(
            cw.at[block, :, pl.ds(start, width)], pieces.at[det],
            piece_send.at[block, k], piece_recv.at[det], det=target,
        )

    def hand_out(block, wait=False):
        def one(k):
            target, copy = piece(block, k)

            @pl.when(target != det)
            def _():
                if wait:
                    copy.wait_send()
                else:
                    copy.start()

        each(per_block, one)

    following = lax.rem(det + 1, n)
    visit = remote(c_ref, vis, vis_send.at[0], vis_recv.at[0], det=following)
    visit_amp = remote(amps.at[0], amps.at[1], vis_send.at[1], vis_recv.at[1], det=following)
    visit.start()
    visit_amp.start()
    keep.wait()
    for half in (0, 1):
        for side in (0, 1):
            pass_on(row, side, half)
    s0[...] = against(c_ref[...], c_ref[...])
    visit.wait_recv()
    own[...] = against(vis[...], c_ref[...])

    @pl.when(row == 0)
    def _():
        sums(0, True)

    @pl.when(row == ring - 1)
    def _():
        sums(1, True)

    hand_out(row)

    def arrive(distance):
        for side in (0, 1):
            block = row - distance if side == 0 else row + distance

            @pl.when((block >= 0) & (block < ring))
            def _():
                along(block, side, 0).wait_recv()
                pass_on(block, side, 0)

        for side in (0, 1):
            block = row - distance if side == 0 else row + distance

            @pl.when((block >= 0) & (block < ring))
            def _():
                along(block, side, 1).wait_recv()
                pass_on(block, side, 1)
                hand_out(block)
                s0[...] += against(cw[block], cw[block])

    def gather_sums(distance):
        @pl.when(row == distance)
        def _():
            sums(0, False)

        @pl.when(row == ring - 1 - distance)
        def _():
            sums(1, False)

    for distance in range(1, ring - 1):
        arrive(distance)
        gather_sums(distance)
    arrive(ring - 1)
    visit_amp.wait_recv()
    amp = amps[0, 0:1, 0:1]
    masks = plan_ref[...].astype(F32)
    weight = amp * amp * masks[0:1, 0:1]
    scaled = (weight * inverse_of(s0[...])).astype(BF16)
    total = jnp.dot(scaled, c_ref[...], preferred_element_type=F32)
    gather_sums(ring - 1)
    weight = amps[1, 0:1, 0:1] * amp * masks[1:2, 0:1]
    correlation = own[...] + sum_in[0] + sum_in[1]
    scaled = (weight * inverse_of(correlation)).astype(BF16)
    total = total + jnp.dot(scaled, vis[...], preferred_element_type=F32)
    folded[det] = total.astype(BF16)

    def to_chip(i):
        target = lax.rem(chip + 1 + i, chips) * 2 + core
        return remote(folded.at[det], folded.at[det], chip_send.at[i], folded_recv.at[det], det=target)

    def to_pair(source):
        return remote(
            folded.at[source], folded.at[source], pair_send.at[source], folded_recv.at[source], det=partner
        )

    each(chips - 1, lambda i: to_chip(i).start())
    to_pair(det).start()

    def landed(source):
        to_pair(source).wait_recv()

    sink = out_ref if width == rows else wide

    def add(source):
        remote(
            cw.at[0, :, pl.ds(0, width)], pieces.at[source], piece_send.at[0, 0], piece_recv.at[source],
            det=partner,
        ).wait_recv()
        sink[...] += gram(pieces[source], folded[source])

    own_start = lax.rem(det, per_block) * rows // width * width
    mine = cw[det // per_block, :, pl.ds(pl.multiple_of(own_start, width), width)]
    sink[...] = gram(mine, folded[det])
    landed(partner)
    add(partner)

    def relay(i):
        other = lax.rem(chip + chips - 1 - i, chips) * 2
        landed(other + core)
        to_pair(other + core).start()
        add(other + core)

    def relayed(i):
        other = lax.rem(chip + chips - 1 - i, chips) * 2
        landed(other + 1 - core)
        add(other + 1 - core)

    each(chips - 1, relay)
    each(chips - 1, relayed)
    if width != rows:
        out_ref[...] = wide[pl.ds(pl.multiple_of(lax.rem(det * rows, width), rows), rows)]

    visit.wait_send()
    visit_amp.wait_send()
    for side in (0, 1):
        for half in (0, 1):
            pass_on(row, side, half, wait=True)

        @pl.when(toward[side])
        def _():
            for k in range(len(chunks)):
                chunk_copy(k, side).wait_send()

    hand_out(row, wait=True)
    for distance in range(1, ring):
        for side in (0, 1):
            block = row - distance if side == 0 else row + distance

            @pl.when((block >= 0) & (block < ring))
            def _():
                for half in (0, 1):
                    pass_on(block, side, half, wait=True)
                hand_out(block, wait=True)

    each(chips - 1, lambda i: to_chip(i).wait_send())
    to_pair(det).wait_send()
    each(chips - 1, lambda i: to_pair(lax.rem(chip + chips - 1 - i, chips) * 2 + core).wait_send())


def on_device(coefficients, amplitudes, plan):
    n, ring = lax.axis_size("det"), lax.axis_size("row")
    if coefficients.shape[0] != 1 or plan.shape[1] != 2:
        raise ValueError("unsupported sizes")
    block = jnp.swapaxes(coefficients, 1, 2)[0]
    orbitals, size = block.shape
    rows = size * ring // n
    width = max(rows, 128)
    dma = pltpu.SemaphoreType.DMA
    return pl.pallas_call(
        functools.partial(kernel, n, ring),
        out_shape=jax.ShapeDtypeStruct((rows, size), F32),
        in_specs=[pl.BlockSpec(memory_space=pltpu.VMEM)] * 3,
        out_specs=pl.BlockSpec(memory_space=pltpu.VMEM),
        scratch_shapes=[
            pltpu.VMEM((ring, orbitals, size), BF16),
            pltpu.VMEM((orbitals, size), BF16),
            pltpu.VMEM((2, 8, 128), F32),
            pltpu.VMEM((orbitals, orbitals), F32),
            pltpu.VMEM((2, orbitals, orbitals), F32),
            pltpu.VMEM((2, orbitals, orbitals), F32),
            pltpu.VMEM((orbitals, orbitals), F32),
            pltpu.VMEM((n, orbitals, width), BF16),
            pltpu.VMEM((n, orbitals, size), BF16),
            pltpu.VMEM((width, size) if width != rows else (8, 128), F32),
            dma, dma((ring, 2, 2)), dma((ring, 2)), dma((2, 4)), dma((2, 4)), dma((2,)), dma((2,)),
            dma((ring, n // ring)), dma((n,)), dma((n // 2,)), dma((n,)), dma((n,)),
        ],
        compiler_params=pltpu.CompilerParams(
            collective_id=0, has_side_effects=True, vmem_limit_bytes=60 * 1024 * 1024
        ),
    )(block, amplitudes.reshape(1, 1), plan.reshape(2, 1))


def solution(mesh):
    placed = (P("det", "row", None), P("det"), P("det", None, None))
    return jax.shard_map(
        on_device, mesh=mesh, in_specs=placed, out_specs=P("det", "row"), check_vma=False
    )
```
